128 devices in a mesh: row: 16 (over y_hi, x, core), col: 8 (over y_lo, z).
Axes of the slice: x: 4, y: 4 (y_hi: 2, y_lo: 2; y = y_hi * 2 + y_lo), z: 4, core: 2. Of those that a mesh axis runs over, the one named last changes fastest.
Arguments:
- gradient: float32 [2048, 14336], P('row', 'col'), may hold values from -6 to 6
- precond: bfloat16 [14336, 14336], P('row', 'col'), as said below
Outputs:
- direction: float32 [2048, 14336], P('row', 'col')
The draws below stay inside these ranges and needn't reach their ends.
Inputs may be any that keep to these rules, and one draw needn't show every extreme that they name: precond is symmetric, and its diagonal is positive and larger than any off-diagonal entry in the same row (the matrix is not diagonally dominant: the off-diagonal entries together outweigh the diagonal).
All inputs are finite; a program needn't handle non-finite values.
Results may differ from the reference program's by a relative error of at most 0.0039.
Values may be sent and summed in bfloat16 or wider, within the bound.
A program may use at most 64 MiB of HBM per device.

```python
import jax
import jax.numpy as jnp
from jax import lax

N = 14336
K = 2048
N_COL = 8


def draw_precond(key, part):
    key_off = jax.random.fold_in(key, 11)
    key_diag = jax.random.fold_in(key, 12)
    raw = jax.random.normal(key_off, (N, N), jnp.float32)
    off_part = (raw + raw.T) * (0.5 / jnp.sqrt(jnp.float32(N)))
    diag_part = jax.random.uniform(key_diag, (N,), jnp.float32, 0.6, 1.6)
    whole = off_part + jnp.diag(diag_part)
    return whole.astype(jnp.bfloat16)


def level_of(rng, dims, shards, low, top_value):
    factor_of = 1.0
    for axis_at, shards_of in shards:
        steps = jax.random.uniform(jax.random.fold_in(jax.random.fold_in(rng, 6), axis_at), (shards_of,), jnp.float32, low / len(shards), top_value / len(shards))
        factor_of = factor_of * jnp.repeat(jnp.exp(steps), dims[axis_at] // shards_of).reshape((-1,) + (1,) * (len(dims) - 1 - axis_at))
    return factor_of


def gaussian(key, dims, deviation, limit, shards=(), kind=jnp.bfloat16):
    drawn = deviation * jax.random.normal(key, dims, jnp.float32)
    if shards:
        drawn = drawn * level_of(key, dims, shards, -0.22, 0.18)
    return jnp.clip(drawn, -limit, limit).astype(kind)


def setup_inputs(seed: int = 0) -> dict:
    key_of = jax.random.split(jax.random.key(seed), 3)
    return {
        "gradient": gaussian(key_of[0], (K, N), 1.0, 6.0, ((0, 16), (1, 8)), jnp.float32),
        "precond": draw_precond(jax.random.fold_in(key_of[2], 71), 0),
    }


def times_factor(operand, precond):
    width = N // N_COL
    count = N // width
    wide = operand.astype(jnp.float32)

    def one_block(block_index):
        columns = lax.dynamic_slice_in_dim(precond, block_index * width, width, 1).astype(jnp.float32)
        return jnp.dot(wide, columns, precision=lax.Precision.HIGHEST)

    stacked = lax.map(one_block, jnp.arange(count, dtype=jnp.int32))
    return jnp.transpose(stacked, (1, 0, 2)).reshape(operand.shape[0], N)


def reference(gradient, precond):
    grad_low = gradient.astype(jnp.bfloat16)
    first = times_factor(grad_low, precond).astype(jnp.bfloat16)
    return times_factor(first, precond)
```

```python
import functools

import jax
import jax.numpy as jnp
from jax import lax
from jax.experimental import pallas as pl
from jax.experimental.pallas import tpu as pltpu
from jax.sharding import PartitionSpec as P

MESH = pl.DeviceIdType.MESH
BF16, F32 = jnp.bfloat16, jnp.float32

W = 64
TILE = 256
RING = 4

GATHER_X, SEND_G, SCATTER_Z, PAIR, GATHER_Z, SCATTER_X, SEND_OUT, KINDS = 0, 4, 5, 11, 12, 16, 22, 23

ORDER = (
    ("enter", -2), ("relay", -1), ("first", 0), ("to_pair", 1), ("second", 3), ("hop1", 0), ("round_first", 1),
    ("hop2", 3), ("relay2", 2), ("end", 4),
)


def kernel(rows, g_hbm, q_hbm, out, g_wide, factor, gath, part, own, hop_s, plus_s, minus_s, hop_r, plus_r,
           minus_r, pair_s, pair_r, mid, part2, own2, hop2_s, plus2_s, minus2_s, hop2_r, plus2_r, minus2_r,
           out_s, out_r, local_sem, core_send, core_recv, ss, rs):
    half_chunks = rows // W
    chunks = 2 * half_chunks
    early = half_chunks // 2
    r, c = lax.axis_index("row"), lax.axis_index("col")
    core = r % 2
    x = (r // 2) % RING
    yh = r // (2 * RING)
    z = c % RING
    yl = c // RING

    def at(yh, x, core, yl, z):
        return ((yh * RING + x) * 2 + core, yl * RING + z)

    xr, xl, xo = (x + 1) % RING, (x + 3) % RING, (x + 2) % RING
    zr, zl, zo = (z + 1) % RING, (z + 3) % RING, (z + 2) % RING
    x_plus, x_minus = at(yh, xr, core, yl, z), at(yh, xl, core, yl, z)
    z_plus, z_minus = at(yh, x, core, yl, zr), at(yh, x, core, yl, zl)
    far = at(1 - yh, x, core, yl, z)
    pair = at(yh, x, core, 1 - yl, z)
    twin = at(yh, x, 1 - core, yl, z)

    depth = q_hbm.shape[0]
    mine = pl.ds(pl.multiple_of(core * depth, depth), depth)
    theirs = pl.ds(pl.multiple_of((1 - core) * depth, depth), depth)
    top, low = pl.ds(0, W // 2), pl.ds(W // 2, W // 2)

    load_g = pltpu.make_async_copy(g_hbm, g_wide, local_sem.at[0])
    load_q = pltpu.make_async_copy(q_hbm, factor.at[mine], local_sem.at[1])
    load_g.start()
    load_q.start()

    barrier = pltpu.get_barrier_semaphore()
    for device in (x_plus, x_minus, z_plus, z_minus, far, pair, twin):
        pl.semaphore_signal(barrier, inc=1, device_id=device, device_id_type=MESH)
    pl.semaphore_wait(barrier, 7)

    share = pltpu.make_async_remote_copy(
        src_ref=q_hbm, dst_ref=factor.at[mine], send_sem=core_send, recv_sem=core_recv,
        device_id=twin, device_id_type=MESH)
    share.start()

    def copy(kind, i, src, dst, device):
        return pltpu.make_async_remote_copy(
            src_ref=src, dst_ref=dst, send_sem=ss.at[kind, i], recv_sem=rs.at[kind, i],
            device_id=device, device_id_type=MESH)

    def gather_send(kind, i, buf, me, plus, minus):
        copy(kind, i, buf.at[i, me], buf.at[i, me], plus).start()
        copy(kind + 1, i, buf.at[i, me], buf.at[i, me], minus).start()

    def gather_relay(kind, i, buf, left, right, plus, minus):
        copy(kind, i, buf.at[i, left], buf.at[i, left], plus).wait_recv()
        copy(kind + 2, i, buf.at[i, left, top], buf.at[i, left, top], plus).start()
        copy(kind + 1, i, buf.at[i, right], buf.at[i, right], minus).wait_recv()
        copy(kind + 3, i, buf.at[i, right, low], buf.at[i, right, low], minus).start()

    def gather_wait(kind, i, buf, across, plus, minus):
        copy(kind + 2, i, buf.at[i, across, top], buf.at[i, across, top], plus).wait_recv()
        copy(kind + 3, i, buf.at[i, across, low], buf.at[i, across, low], minus).wait_recv()

    def scatter_send(kind, i, p, mine_f, hs, ps, ms, hr, pr, mr, me, left, right, across, plus, minus):
        hs[i] = p[across].astype(BF16)
        copy(kind, i, hs.at[i, top], hr.at[i, top], plus).start()
        copy(kind + 1, i, hs.at[i, low], hr.at[i, low], minus).start()
        ps[i, W // 2:] = p[right, W // 2:].astype(BF16)
        copy(kind + 2, i, ps.at[i, low], pr.at[i, low], plus).start()
        ms[i, : W // 2] = p[left, : W // 2].astype(BF16)
        copy(kind + 3, i, ms.at[i, top], mr.at[i, top], minus).start()
        mine_f[i] = p[me]

    def scatter_hop(kind, i, p, hs, ps, ms, hr, pr, mr, left, right, plus, minus):
        copy(kind, i, hs.at[i, top], hr.at[i, top], plus).wait_recv()
        ps[i, : W // 2] = (p[right, : W // 2] + hr[i, : W // 2].astype(F32)).astype(BF16)
        copy(kind + 4, i, ps.at[i, top], pr.at[i, top], plus).start()
        copy(kind + 1, i, hs.at[i, low], hr.at[i, low], minus).wait_recv()
        ms[i, W // 2:] = (p[left, W // 2:] + hr[i, W // 2:].astype(F32)).astype(BF16)
        copy(kind + 5, i, ms.at[i, low], mr.at[i, low], minus).start()

    def scatter_wait(kind, i, mine_f, ps, ms, pr, mr, plus, minus):
        copy(kind + 2, i, ps.at[i, low], pr.at[i, low], plus).wait_recv()
        copy(kind + 3, i, ms.at[i, top], mr.at[i, top], minus).wait_recv()
        copy(kind + 4, i, ps.at[i, top], pr.at[i, top], plus).wait_recv()
        copy(kind + 5, i, ms.at[i, low], mr.at[i, low], minus).wait_recv()
        return mine_f[i] + pr[i].astype(F32) + mr[i].astype(F32)

    load_g.wait()
    for q in range(half_chunks):
        i = q if q < early else half_chunks + q
        gath[i, x] = g_wide[q * W:(q + 1) * W].astype(BF16)
        gather_send(GATHER_X, i, gath, x, x_plus, x_minus)
        copy(SEND_G, early + q, gath.at[i, x], gath.at[early + q, x], far).start()
    load_q.wait()

    width = factor.shape[1]

    def stage(step, lag, fn):
        i = step - lag

        @pl.when((i >= 0) & (i < chunks))
        def _():
            fn(i)

    def is_far(i):
        return (i >= early) & (i < early + half_chunks)

    def enter(i):
        @pl.when(is_far(i))
        def _():
            copy(SEND_G, i, gath.at[i, x], gath.at[i, x], far).wait_recv()
            gather_send(GATHER_X, i, gath, x, x_plus, x_minus)

    def relay(i):
        gather_relay(GATHER_X, i, gath, xl, xr, x_plus, x_minus)

    def first(i):
        gather_wait(GATHER_X, i, gath, xo, x_plus, x_minus)

        @pl.when(i == 0)
        def _():
            pltpu.make_async_remote_copy(
                src_ref=q_hbm, dst_ref=factor.at[theirs], send_sem=core_send, recv_sem=core_recv,
                device_id=twin, device_id_type=MESH).wait_recv()

        lhs = gath[i].reshape(RING * W, width)
        for t in range(0, width, TILE):
            value = lax.dot_general(lhs, factor[t:t + TILE, :], (((1,), (1,)), ((), ())), preferred_element_type=F32)
            part[:, :, t:t + TILE] = value.reshape(RING, W, TILE)
        scatter_send(SCATTER_Z, i, part, own, hop_s, plus_s, minus_s, hop_r, plus_r, minus_r,
                     z, zl, zr, zo, z_plus, z_minus)

    def hop1(i):
        scatter_hop(SCATTER_Z, i, part, hop_s, plus_s, minus_s, hop_r, plus_r, minus_r, zl, zr, z_plus, z_minus)

    def to_pair(i):
        value = scatter_wait(SCATTER_Z, i, own, plus_s, minus_s, plus_r, minus_r, z_plus, z_minus)
        own[i] = value
        pair_s[i] = value.astype(BF16)
        copy(PAIR, i, pair_s.at[i], pair_r.at[i], pair).start()

    def round_first(i):
        copy(PAIR, i, pair_s.at[i], pair_r.at[i], pair).wait_recv()
        mid[i, z] = (own[i] + pair_r[i].astype(F32)).astype(BF16)
        gather_send(GATHER_Z, i, mid, z, z_plus, z_minus)

    def relay2(i):
        gather_relay(GATHER_Z, i, mid, zl, zr, z_plus, z_minus)

    def second(i):
        gather_wait(GATHER_Z, i, mid, zo, z_plus, z_minus)
        lhs = mid[i].reshape(RING * W, width)
        for t in range(0, width, TILE):
            value = jnp.dot(lhs, factor[:, t:t + TILE], preferred_element_type=F32)
            part2[:, :, t:t + TILE] = value.reshape(RING, W, TILE)
        scatter_send(SCATTER_X, i, part2, own2, hop2_s, plus2_s, minus2_s, hop2_r, plus2_r, minus2_r,
                     x, xl, xr, xo, x_plus, x_minus)

    def hop2(i):
        scatter_hop(SCATTER_X, i, part2, hop2_s, plus2_s, minus2_s, hop2_r, plus2_r, minus2_r,
                    xl, xr, x_plus, x_minus)

    def end(i):
        value = scatter_wait(SCATTER_X, i, own2, plus2_s, minus2_s, plus2_r, minus2_r, x_plus, x_minus)

        @pl.when(is_far(i))
        def _():
            out_s[i - early] = value.astype(BF16)
            copy(SEND_OUT, i - early, out_s.at[i - early], out_r.at[i - early], far).start()

        @pl.when(jnp.logical_not(is_far(i)))
        def _():
            q = jnp.where(i < early, i, i - half_chunks)
            out[pl.ds(pl.multiple_of(q * W, W), W), :] = value

    stages = {
        "enter": enter, "relay": relay, "first": first, "hop1": hop1, "to_pair": to_pair,
        "round_first": round_first, "relay2": relay2, "second": second, "hop2": hop2, "end": end,
    }
    lags = [lag for _, lag in ORDER]

    def loop(step, carry):
        for name, lag in ORDER:
            stage(step, lag, stages[name])
        return carry

    lax.fori_loop(min(lags), chunks + max(lags), loop, 0)

    for q in range(half_chunks):
        copy(SEND_OUT, q, out_s.at[q], out_r.at[q], far).wait_recv()
        out[q * W:(q + 1) * W] += out_r[q].astype(F32)

    share.wait_send()

    def drain(i, carry):
        for kind, buf in ((GATHER_X, gath), (GATHER_Z, mid)):
            for k, piece in enumerate((buf.at[i, 0], buf.at[i, 0], buf.at[i, 0, top], buf.at[i, 0, low])):
                copy(kind + k, i, piece, piece, x_plus).wait_send()
        for kind in (SCATTER_Z, SCATTER_X):
            for k in range(6):
                copy(kind + k, i, hop_s.at[i, top], hop_s.at[i, top], x_plus).wait_send()
        copy(PAIR, i, pair_s.at[i], pair_s.at[i], pair).wait_send()

        @pl.when(i < half_chunks)
        def _():
            copy(SEND_G, early + i, pair_s.at[i], pair_s.at[i], far).wait_send()
            copy(SEND_OUT, i, out_s.at[i], out_s.at[i], far).wait_send()

        return carry

    lax.fori_loop(0, chunks, drain, 0)


def local(gradient, precond):
    rows, width = gradient.shape
    chunks = 2 * rows // W
    block = pltpu.VMEM((chunks, W, width), BF16)
    wide = pltpu.VMEM((chunks, W, width), F32)
    ring = pltpu.VMEM((chunks, RING, W, width), BF16)
    part = pltpu.VMEM((RING, W, width), F32)
    out_block = pltpu.VMEM((chunks // 2, W, width), BF16)
    return pl.pallas_call(
        functools.partial(kernel, rows),
        out_shape=jax.ShapeDtypeStruct((rows, width), F32),
        in_specs=[pl.BlockSpec(memory_space=pl.ANY)] * 2,
        out_specs=pl.BlockSpec(memory_space=pltpu.VMEM),
        scratch_shapes=[
            pltpu.VMEM((rows, width), F32),
            pltpu.VMEM((2 * precond.shape[0], width), BF16),
            ring, part, wide, block, block, block, block, block, block, block, block,
            ring, part, wide, block, block, block, block, block, block,
            out_block, out_block,
            pltpu.SemaphoreType.DMA((2,)),
            pltpu.SemaphoreType.DMA,
            pltpu.SemaphoreType.DMA,
            pltpu.SemaphoreType.DMA((KINDS, chunks)),
            pltpu.SemaphoreType.DMA((KINDS, chunks)),
        ],
        compiler_params=pltpu.CompilerParams(
            collective_id=0, has_side_effects=True, vmem_limit_bytes=60 * 1024 * 1024
        ),
    )(gradient, precond)


def solution(mesh):
    placed = (P("row", "col"), P("row", "col"))
    return jax.shard_map(
        local, mesh=mesh, in_specs=placed, out_specs=P("row", "col"), check_vma=False
    )
```

```python
import functools

import jax
import jax.numpy as jnp
from jax import lax
from jax.experimental import pallas as pl
from jax.experimental.pallas import tpu as pltpu
from jax.sharding import PartitionSpec as P

MESH = pl.DeviceIdType.MESH
BF16, F32 = jnp.bfloat16, jnp.float32

W = 32
TILE = 256
SPAN = 30
RING = 4

GATHER_X, SEND_G, SCATTER_Z, PAIR, GATHER_Z, SCATTER_X, SEND_OUT, KINDS = 0, 4, 5, 11, 12, 16, 22, 23

ORDER = (
    "enter",
    "first",
    "round_first",
    "relay",
    "to_pair",
    "hop2",
    "second",
    "hop1",
    "relay2",
    "end",
)
STEPS = {
    "enter": (0, 1, 2, 3, 4, 5, 6, 7),
    "first": (3, 4, 7, 8, 12, 14, 15, 17),
    "round_first": (10, 11, 12, 14, 20, 23, 27, 28),
    "relay": (1, 2, 3, 4, 7, 8, 9, 10),
    "to_pair": (8, 9, 10, 13, 19, 21, 25, 26),
    "hop2": (18, 21, 22, 26, 30, 31, 33, 34),
    "second": (15, 16, 19, 24, 27, 29, 31, 32),
    "hop1": (4, 7, 8, 9, 14, 16, 20, 22),
    "relay2": (12, 13, 14, 17, 24, 26, 29, 30),
    "end": (19, 22, 23, 28, 31, 32, 34, 35),
}


def kernel(rows, g_hbm, q_hbm, out, g_wide, factor, gath, part, hop_s, plus_s, minus_s, hop_r, plus_r,
           minus_r, pair_s, pair_r, mid, part2, hop2_s, plus2_s, minus2_s, hop2_r, plus2_r, minus2_r,
           out_s, out_r, local_sem, core_send, core_recv, ss, rs):
    half_chunks = rows // W
    chunks = 2 * half_chunks
    early = half_chunks // 2
    r, c = lax.axis_index("row"), lax.axis_index("col")
    core = r % 2
    x = (r // 2) % RING
    yh = r // (2 * RING)
    z = c % RING
    yl = c // RING

    def at(yh, x, core, yl, z):
        return ((yh * RING + x) * 2 + core, yl * RING + z)

    xr, xl, xo = (x + 1) % RING, (x + 3) % RING, (x + 2) % RING
    zr, zl, zo = (z + 1) % RING, (z + 3) % RING, (z + 2) % RING
    x_plus, x_minus = at(yh, xr, core, yl, z), at(yh, xl, core, yl, z)
    z_plus, z_minus = at(yh, x, core, yl, zr), at(yh, x, core, yl, zl)
    far = at(1 - yh, x, core, yl, z)
    pair = at(yh, x, core, 1 - yl, z)
    twin = at(yh, x, 1 - core, yl, z)

    depth = q_hbm.shape[0]
    mine = pl.ds(pl.multiple_of(core * depth, depth), depth)
    theirs = pl.ds(pl.multiple_of((1 - core) * depth, depth), depth)
    top, low = pl.ds(0, W // 2), pl.ds(W // 2, W // 2)

    load_g = pltpu.make_async_copy(g_hbm, g_wide, local_sem.at[0])
    load_q = pltpu.make_async_copy(q_hbm, factor.at[mine], local_sem.at[1])
    load_g.start()
    load_q.start()

    barrier = pltpu.get_barrier_semaphore()
    for device in (x_plus, x_minus, z_plus, z_minus, far, pair, twin):
        pl.semaphore_signal(barrier, inc=1, device_id=device, device_id_type=MESH)
    pl.semaphore_wait(barrier, 7)

    share = pltpu.make_async_remote_copy(
        src_ref=q_hbm, dst_ref=factor.at[mine], send_sem=core_send, recv_sem=core_recv,
        device_id=twin, device_id_type=MESH)
    share.start()

    def copy(kind, i, src, dst, device):
        return pltpu.make_async_remote_copy(
            src_ref=src, dst_ref=dst, send_sem=ss.at[kind, i], recv_sem=rs.at[kind, i],
            device_id=device, device_id_type=MESH)

    def gather_send(kind, i, buf, me, plus, minus):
        copy(kind, i, buf.at[i, me], buf.at[i, me], plus).start()
        copy(kind + 1, i, buf.at[i, me], buf.at[i, me], minus).start()

    def gather_relay(kind, i, buf, left, right, plus, minus):
        copy(kind, i, buf.at[i, left], buf.at[i, left], plus).wait_recv()
        copy(kind + 2, i, buf.at[i, left, top], buf.at[i, left, top], plus).start()
        copy(kind + 1, i, buf.at[i, right], buf.at[i, right], minus).wait_recv()
        copy(kind + 3, i, buf.at[i, right, low], buf.at[i, right, low], minus).start()

    def gather_wait(kind, i, buf, across, plus, minus):
        copy(kind + 2, i, buf.at[i, across, top], buf.at[i, across, top], plus).wait_recv()
        copy(kind + 3, i, buf.at[i, across, low], buf.at[i, across, low], minus).wait_recv()

    def scatter_send(kind, i, p, hs, ps, ms, hr, pr, mr, left, right, across, plus, minus):
        hs[i] = p[i, across].astype(BF16)
        copy(kind, i, hs.at[i, top], hr.at[i, top], plus).start()
        copy(kind + 1, i, hs.at[i, low], hr.at[i, low], minus).start()
        ps[i, W // 2:] = p[i, right, W // 2:].astype(BF16)
        copy(kind + 2, i, ps.at[i, low], pr.at[i, low], plus).start()
        ms[i, : W // 2] = p[i, left, : W // 2].astype(BF16)
        copy(kind + 3, i, ms.at[i, top], mr.at[i, top], minus).start()

    def scatter_hop(kind, i, p, hs, ps, ms, hr, pr, mr, left, right, plus, minus):
        copy(kind, i, hs.at[i, top], hr.at[i, top], plus).wait_recv()
        ps[i, : W // 2] = (p[i, right, : W // 2] + hr[i, : W // 2].astype(F32)).astype(BF16)
        copy(kind + 4, i, ps.at[i, top], pr.at[i, top], plus).start()
        copy(kind + 1, i, hs.at[i, low], hr.at[i, low], minus).wait_recv()
        ms[i, W // 2:] = (p[i, left, W // 2:] + hr[i, W // 2:].astype(F32)).astype(BF16)
        copy(kind + 5, i, ms.at[i, low], mr.at[i, low], minus).start()

    def scatter_wait(kind, i, p, me, ps, ms, pr, mr, plus, minus):
        copy(kind + 2, i, ps.at[i, low], pr.at[i, low], plus).wait_recv()
        copy(kind + 3, i, ms.at[i, top], mr.at[i, top], minus).wait_recv()
        copy(kind + 4, i, ps.at[i, top], pr.at[i, top], plus).wait_recv()
        copy(kind + 5, i, ms.at[i, low], mr.at[i, low], minus).wait_recv()
        return p[i, me] + pr[i].astype(F32) + mr[i].astype(F32)

    load_g.wait()
    for q in range(half_chunks):
        i = q if q < early else half_chunks + q
        gath[i, x] = g_wide[q * W:(q + 1) * W].astype(BF16)
        if i == 0:
            gather_send(GATHER_X, i, gath, x, x_plus, x_minus)
        copy(SEND_G, early + q, gath.at[i, x], gath.at[early + q, x], far).start()
    load_q.wait()

    width = factor.shape[1]

    def is_far(i):
        return (i >= early) & (i < early + half_chunks)

    def enter(i):
        @pl.when(is_far(i))
        def _():
            copy(SEND_G, i, gath.at[i, x], gath.at[i, x], far).wait_recv()

        @pl.when(i > 0)
        def _():
            gather_send(GATHER_X, i, gath, x, x_plus, x_minus)

    def relay(i):
        gather_relay(GATHER_X, i, gath, xl, xr, x_plus, x_minus)

    def first(i):
        gather_wait(GATHER_X, i, gath, xo, x_plus, x_minus)

        @pl.when(i == 0)
        def _():
            pltpu.make_async_remote_copy(
                src_ref=q_hbm, dst_ref=factor.at[theirs], send_sem=core_send, recv_sem=core_recv,
                device_id=twin, device_id_type=MESH).wait_recv()

        lhs = gath[i].reshape(RING * W, width)
        for t in range(0, width, TILE):
            value = lax.dot_general(lhs, factor[t:t + TILE, :], (((1,), (1,)), ((), ())), preferred_element_type=F32)
            part[i, :, :, t:t + TILE] = value.reshape(RING, W, TILE)
        scatter_send(SCATTER_Z, i, part, hop_s, plus_s, minus_s, hop_r, plus_r, minus_r,
                     zl, zr, zo, z_plus, z_minus)

    def hop1(i):
        scatter_hop(SCATTER_Z, i, part, hop_s, plus_s, minus_s, hop_r, plus_r, minus_r, zl, zr, z_plus, z_minus)

    def to_pair(i):
        value = scatter_wait(SCATTER_Z, i, part, z, plus_s, minus_s, plus_r, minus_r, z_plus, z_minus)
        part[i, z] = value
        pair_s[i] = value.astype(BF16)
        copy(PAIR, i, pair_s.at[i], pair_r.at[i], pair).start()

    def round_first(i):
        copy(PAIR, i, pair_s.at[i], pair_r.at[i], pair).wait_recv()
        mid[i, z] = (part[i, z] + pair_r[i].astype(F32)).astype(BF16)
        gather_send(GATHER_Z, i, mid, z, z_plus, z_minus)

    def relay2(i):
        gather_relay(GATHER_Z, i, mid, zl, zr, z_plus, z_minus)

    def second(i):
        gather_wait(GATHER_Z, i, mid, zo, z_plus, z_minus)
        lhs = mid[i].reshape(RING * W, width)
        for t in range(0, width, TILE):
            value = jnp.dot(lhs, factor[:, t:t + TILE], preferred_element_type=F32)
            part2[i, :, :, t:t + TILE] = value.reshape(RING, W, TILE)
        scatter_send(SCATTER_X, i, part2, hop2_s, plus2_s, minus2_s, hop2_r, plus2_r, minus2_r,
                     xl, xr, xo, x_plus, x_minus)

    def hop2(i):
        scatter_hop(SCATTER_X, i, part2, hop2_s, plus2_s, minus2_s, hop2_r, plus2_r, minus2_r,
                    xl, xr, x_plus, x_minus)

    def end(i):
        value = scatter_wait(SCATTER_X, i, part2, x, plus2_s, minus2_s, plus2_r, minus2_r, x_plus, x_minus)

        @pl.when(is_far(i))
        def _():
            out_s[i - early] = value.astype(BF16)
            copy(SEND_OUT, i - early, out_s.at[i - early], out_r.at[i - early], far).start()

        @pl.when(jnp.logical_not(is_far(i)))
        def _():
            q = jnp.where(i < early, i, i - half_chunks)
            out[pl.ds(pl.multiple_of(q * W, W), W), :] = value

    stages = {
        "enter": enter, "relay": relay, "first": first, "hop1": hop1, "to_pair": to_pair,
        "round_first": round_first, "relay2": relay2, "second": second, "hop2": hop2, "end": end,
    }
    total = 1 + max(max(at_steps) for at_steps in STEPS.values())
    words = [
        [sum(1 << (t - w) for t in STEPS[name] if w <= t < w + SPAN) for w in range(0, total, SPAN)]
        for name in ORDER
    ]

    def loop(step, carry):
        bits, counts = carry
        next_bits, next_counts = [], []
        for name, word, bit, count in zip(ORDER, words, bits, counts):
            for w in range(1, len(word)):
                bit = jnp.where(step == w * SPAN, word[w], bit)
            on = bit % 2

            @pl.when(on == 1)
            def _():
                stages[name](count)

            next_bits.append(bit // 2)
            next_counts.append(count + on)
        return tuple(next_bits), tuple(next_counts)

    start = tuple(jnp.int32(word[0]) for word in words), tuple(jnp.int32(0) for _ in words)
    lax.fori_loop(0, total, loop, start)

    for q in range(half_chunks):
        copy(SEND_OUT, q, out_s.at[q], out_r.at[q], far).wait_recv()
        out[q * W:(q + 1) * W] += out_r[q].astype(F32)

    share.wait_send()

    def drain(i, carry):
        for kind, buf in ((GATHER_X, gath), (GATHER_Z, mid)):
            for k, piece in enumerate((buf.at[i, 0], buf.at[i, 0], buf.at[i, 0, top], buf.at[i, 0, low])):
                copy(kind + k, i, piece, piece, x_plus).wait_send()
        for kind in (SCATTER_Z, SCATTER_X):
            for k in range(6):
                copy(kind + k, i, hop_s.at[i, top], hop_s.at[i, top], x_plus).wait_send()
        copy(PAIR, i, pair_s.at[i], pair_s.at[i], pair).wait_send()

        @pl.when(i < half_chunks)
        def _():
            copy(SEND_G, early + i, pair_s.at[i], pair_s.at[i], far).wait_send()
            copy(SEND_OUT, i, out_s.at[i], out_s.at[i], far).wait_send()

        return carry

    lax.fori_loop(0, chunks, drain, 0)


def local(gradient, precond):
    rows, width = gradient.shape
    chunks = 2 * rows // W
    block = pltpu.VMEM((chunks, W, width), BF16)
    ring = pltpu.VMEM((chunks, RING, W, width), BF16)
    part = pltpu.VMEM((chunks, RING, W, width), F32)
    out_block = pltpu.VMEM((chunks // 2, W, width), BF16)
    return pl.pallas_call(
        functools.partial(kernel, rows),
        out_shape=jax.ShapeDtypeStruct((rows, width), F32),
        in_specs=[pl.BlockSpec(memory_space=pl.ANY)] * 2,
        out_specs=pl.BlockSpec(memory_space=pltpu.VMEM),
        scratch_shapes=[
            pltpu.VMEM((rows, width), F32),
            pltpu.VMEM((2 * precond.shape[0], width), BF16),
            ring, part, block, block, block, block, block, block, block, block,
            ring, part, block, block, block, block, block, block,
            out_block, out_block,
            pltpu.SemaphoreType.DMA((2,)),
            pltpu.SemaphoreType.DMA,
            pltpu.SemaphoreType.DMA,
            pltpu.SemaphoreType.DMA((KINDS, chunks)),
            pltpu.SemaphoreType.DMA((KINDS, chunks)),
        ],
        compiler_params=pltpu.CompilerParams(
            collective_id=0, has_side_effects=True, vmem_limit_bytes=60 * 1024 * 1024
        ),
    )(gradient, precond)


def solution(mesh):
    placed = (P("row", "col"), P("row", "col"))
    return jax.shard_map(
        local, mesh=mesh, in_specs=placed, out_specs=P("row", "col"), check_vma=False
    )
```

```python
import functools

import jax
import jax.numpy as jnp
from jax import lax
from jax.experimental import pallas as pl
from jax.experimental.pallas import tpu as pltpu
from jax.sharding import PartitionSpec as P

MESH = pl.DeviceIdType.MESH
BF16, F32 = jnp.bfloat16, jnp.float32

W = 32
TILE = 256
RING = 4
EARLY = 2
FLIP = (3,)
PARTS = 4
SPAN = 30

GATHER_X, SEND_G, SCATTER_Z, PAIR, GATHER_Z, SCATTER_X, SEND_OUT, PRE, POST, KINDS = 0, 6, 7, 13, 14, 20, 26, 27, 28, 29

ORDER = (
    "enter", "to_pair", "relay", "relay2", "hop2",
    "first", "hop1", "merge", "round_first", "second",
    "end", "spread",
)
STEPS = {
    "enter": (0, 1, 2, 3, 7, 10, 11, 12),
    "to_pair": (8, 11, 12, 17, 21, 22, 25, 27),
    "relay": (1, 2, 4, 5, 9, 12, 13, 15),
    "relay2": (12, 18, 19, 20, 26, 27, 30, 31),
    "hop2": (17, 25, 27, 28, 31, 33, 36, 37),
    "first": (3, 6, 7, 8, 11, 16, 21, 22),
    "hop1": (5, 8, 9, 13, 14, 18, 23, 24),
    "merge": (12,),
    "round_first": (10, 12, 15, 23, 25, 27, 29),
    "second": (15, 21, 24, 26, 28, 29, 33, 34),
    "end": (22, 27, 31, 32, 34, 35, 37, 38),
    "spread": (22,),
}


def pick(count, items):
    value = jnp.int32(items[0])
    for k in range(1, len(items)):
        value = jnp.where(count == k, items[k], value)
    return value


def kernel(rows, g_hbm, q_hbm, out, g_wide, factor, factor_t, gath, part, hop_s, plus_s, minus_s, hop_r, plus_r,
           minus_r, pair_s, pair_r, mid, part2, hop2_s, plus2_s, minus2_s, hop2_r, plus2_r, minus2_r,
           out_s, out_r, pre_s, pre_r, total_v, local_sem, core_send, core_recv, ss, rs):
    half_chunks = rows // W
    chunks = 2 * half_chunks
    width = factor.shape[1]
    r, c = lax.axis_index("row"), lax.axis_index("col")
    core = r % 2
    x = (r // 2) % RING
    yh = r // (2 * RING)
    z = c % RING
    yl = c // RING

    def at(yh, x, core, yl, z):
        return ((yh * RING + x) * 2 + core, yl * RING + z)

    xr, xl, xo = (x + 1) % RING, (x + 3) % RING, (x + 2) % RING
    zr, zl, zo = (z + 1) % RING, (z + 3) % RING, (z + 2) % RING
    x_plus, x_minus = at(yh, xr, core, yl, z), at(yh, xl, core, yl, z)
    z_plus, z_minus = at(yh, x, core, yl, zr), at(yh, x, core, yl, zl)
    far = at(1 - yh, x, core, yl, z)
    pair = at(yh, x, core, 1 - yl, z)
    twin = at(yh, x, 1 - core, yl, z)

    depth = q_hbm.shape[0]
    mine = pl.ds(pl.multiple_of(core * depth, depth), depth)
    theirs = pl.ds(pl.multiple_of((1 - core) * depth, depth), depth)
    lo, hi = pl.ds(0, width // 2), pl.ds(width // 2, width // 2)
    whole = pl.ds(0, W)
    kept = pl.ds(pl.multiple_of(yl * (W // 2), W // 2), W // 2)
    given = pl.ds(pl.multiple_of((1 - yl) * (W // 2), W // 2), W // 2)

    load_g = pltpu.make_async_copy(g_hbm, g_wide, local_sem.at[0])
    load_q = pltpu.make_async_copy(q_hbm, factor.at[mine], local_sem.at[1])
    load_g.start()
    load_q.start()

    barrier = pltpu.get_barrier_semaphore()
    for device in (x_plus, x_minus, z_plus, z_minus, far, pair, twin):
        pl.semaphore_signal(barrier, inc=1, device_id=device, device_id_type=MESH)
    pl.semaphore_wait(barrier, 7)

    def factor_copy(side):
        return pltpu.make_async_remote_copy(
            src_ref=q_hbm, dst_ref=factor.at[side], send_sem=core_send, recv_sem=core_recv,
            device_id=twin, device_id_type=MESH)

    factor_copy(mine).start()

    def copy(kind, i, src, dst, device):
        return pltpu.make_async_remote_copy(
            src_ref=src, dst_ref=dst, send_sem=ss.at[kind, i], recv_sem=rs.at[kind, i],
            device_id=device, device_id_type=MESH)

    def gather_send(kind, i, buf, me, plus, minus, part_rows=whole):
        for k, cols, device in ((0, lo, plus), (1, hi, minus), (2, hi, plus), (3, lo, minus)):
            piece = buf.at[i, me, part_rows, cols]
            copy(kind + k, i, piece, piece, device).start()

    def gather_relay(kind, i, buf, left, right, plus, minus, part_rows=whole):
        for k, block, cols, device in ((0, left, lo, plus), (1, right, hi, minus)):
            piece = buf.at[i, block, part_rows, cols]
            copy(kind + k, i, piece, piece, device).wait_recv()
            copy(kind + 4 + k, i, piece, piece, device).start()

    def gather_wait(kind, i, buf, left, right, across, plus, minus, part_rows=whole):
        for k, block, cols in ((2, left, hi), (3, right, lo), (4, across, lo), (5, across, hi)):
            piece = buf.at[i, block, part_rows, cols]
            copy(kind + k, i, piece, piece, plus).wait_recv()

    def scatter_send(kind, i, p, hs, ps, ms, hr, pr, mr, left, right, across, plus, minus, part_rows=whole):
        hs[i, part_rows] = p[i % PARTS, across, part_rows].astype(BF16)
        copy(kind, i, hs.at[i, part_rows, lo], hr.at[i, part_rows, lo], plus).start()
        copy(kind + 1, i, hs.at[i, part_rows, hi], hr.at[i, part_rows, hi], minus).start()
        ps[i, part_rows, hi] = p[i % PARTS, right, part_rows, hi].astype(BF16)
        copy(kind + 2, i, ps.at[i, part_rows, hi], pr.at[i, part_rows, hi], plus).start()
        ms[i, part_rows, lo] = p[i % PARTS, left, part_rows, lo].astype(BF16)
        copy(kind + 3, i, ms.at[i, part_rows, lo], mr.at[i, part_rows, lo], minus).start()

    def scatter_hop(kind, i, p, hs, ps, ms, hr, pr, mr, left, right, plus, minus, part_rows=whole):
        copy(kind, i, hs.at[i, part_rows, lo], hr.at[i, part_rows, lo], plus).wait_recv()
        ps[i, part_rows, lo] = (p[i % PARTS, right, part_rows, lo] + hr[i, part_rows, lo].astype(F32)).astype(BF16)
        copy(kind + 4, i, ps.at[i, part_rows, lo], pr.at[i, part_rows, lo], plus).start()
        copy(kind + 1, i, hs.at[i, part_rows, hi], hr.at[i, part_rows, hi], minus).wait_recv()
        ms[i, part_rows, hi] = (p[i % PARTS, left, part_rows, hi] + hr[i, part_rows, hi].astype(F32)).astype(BF16)
        copy(kind + 5, i, ms.at[i, part_rows, hi], mr.at[i, part_rows, hi], minus).start()

    def scatter_wait(kind, i, p, me, pr, mr, plus, part_rows=whole):
        for k, buf, cols in ((2, pr, hi), (3, mr, lo), (4, pr, lo), (5, mr, hi)):
            piece = buf.at[i, part_rows, cols]
            copy(kind + k, i, piece, piece, plus).wait_recv()
        return p[i % PARTS, me, part_rows] + pr[i, part_rows].astype(F32) + mr[i, part_rows].astype(F32)

    def is_far(i):
        return (i >= EARLY) & (i < EARLY + half_chunks)

    def is_flip(i):
        flag = i < 0
        for f in FLIP:
            flag = flag | (i == f)
        return flag

    def flip_slot(i):
        slot = jnp.int32(0)
        for f in FLIP[1:]:
            slot = slot + (i >= f).astype(jnp.int32)
        return slot

    def choose(flag, yes, no):
        pl.when(flag)(yes)
        pl.when(jnp.logical_not(flag))(no)

    load_g.wait()
    for q in range(half_chunks):
        i = q if q < EARLY else half_chunks + q
        gath[i, x] = g_wide[q * W:(q + 1) * W].astype(BF16)
        if i == 0:
            gather_send(GATHER_X, i, gath, x, x_plus, x_minus)
        copy(SEND_G, EARLY + q, gath.at[i, x], gath.at[EARLY + q, x], far).start()
    load_q.wait()
    factor_t[:, mine] = factor[mine, :].T

    def enter(i):
        @pl.when(is_far(i))
        def _():
            copy(SEND_G, i, gath.at[i, x], gath.at[i, x], far).wait_recv()

        @pl.when(i > 0)
        def _():
            gather_send(GATHER_X, i, gath, x, x_plus, x_minus)

    def relay(i):
        gather_relay(GATHER_X, i, gath, xl, xr, x_plus, x_minus)

    def z_send(i, part_rows):
        scatter_send(SCATTER_Z, i, part, hop_s, plus_s, minus_s, hop_r, plus_r, minus_r,
                     zl, zr, zo, z_plus, z_minus, part_rows)

    def first(i):
        gather_wait(GATHER_X, i, gath, xl, xr, xo, x_plus, x_minus)

        @pl.when(i == 0)
        def _():
            factor_copy(theirs).wait_recv()
            lhs = gath[0].reshape(RING * W, width)
            for t in range(0, width, TILE):
                value = lax.dot_general(
                    lhs, factor[t:t + TILE, :], (((1,), (1,)), ((), ())), preferred_element_type=F32)
                part[0, :, :, t:t + TILE] = value.reshape(RING, W, TILE)
            z_send(0, whole)
            factor_t[:, theirs] = factor[theirs, :].T

        @pl.when(i > 0)
        def _():
            lhs = gath[i].reshape(RING * W, width)
            for t in range(0, width, TILE):
                value = jnp.dot(lhs, factor_t[:, t:t + TILE], preferred_element_type=F32)
                part[i % PARTS, :, :, t:t + TILE] = value.reshape(RING, W, TILE)

            def exchange():
                slot = flip_slot(i)
                pre_s[slot] = part[i % PARTS, :, given].astype(BF16)
                copy(PRE, slot, pre_s.at[slot], pre_r.at[slot], pair).start()

            choose(is_flip(i), exchange, lambda: z_send(i, whole))

    def merge(count):
        i = pick(count, FLIP)
        copy(PRE, count, pre_s.at[count], pre_r.at[count], pair).wait_recv()
        part[i % PARTS, :, kept] += pre_r[count].astype(F32)
        z_send(i, kept)

    def hop1(i):
        def run(part_rows):
            scatter_hop(SCATTER_Z, i, part, hop_s, plus_s, minus_s, hop_r, plus_r, minus_r,
                        zl, zr, z_plus, z_minus, part_rows)

        choose(is_flip(i), lambda: run(kept), lambda: run(whole))

    def to_pair(i):
        def flipped():
            value = scatter_wait(SCATTER_Z, i, part, z, plus_r, minus_r, z_plus, kept)
            mid[i, z, kept] = value.astype(BF16)
            gather_send(GATHER_Z, i, mid, z, z_plus, z_minus, kept)

        def plain():
            value = scatter_wait(SCATTER_Z, i, part, z, plus_r, minus_r, z_plus)
            part[i % PARTS, z] = value
            pair_s[i] = value.astype(BF16)
            copy(PAIR, i, pair_s.at[i], pair_r.at[i], pair).start()

        choose(is_flip(i), flipped, plain)

    def round_first(count):
        i = pick(count, [k for k in range(chunks) if k not in FLIP])
        copy(PAIR, i, pair_s.at[i], pair_r.at[i], pair).wait_recv()
        mid[i, z] = (part[i % PARTS, z] + pair_r[i].astype(F32)).astype(BF16)
        gather_send(GATHER_Z, i, mid, z, z_plus, z_minus)

    def relay2(i):
        def run(part_rows):
            gather_relay(GATHER_Z, i, mid, zl, zr, z_plus, z_minus, part_rows)

        choose(is_flip(i), lambda: run(kept), lambda: run(whole))

    def spread(count):
        i = pick(count, FLIP)
        gather_wait(GATHER_Z, i, mid, zl, zr, zo, z_plus, z_minus, kept)
        copy(POST, count, mid.at[i, :, kept], mid.at[i, :, kept], pair).start()

    def second(i):
        def flipped():
            piece = mid.at[i, :, given]
            copy(POST, flip_slot(i), piece, piece, pair).wait_recv()

        choose(is_flip(i), flipped, lambda: gather_wait(GATHER_Z, i, mid, zl, zr, zo, z_plus, z_minus))
        lhs = mid[i].reshape(RING * W, width)
        for t in range(0, width, TILE):
            value = jnp.dot(lhs, factor[:, t:t + TILE], preferred_element_type=F32)
            part2[i % PARTS, :, :, t:t + TILE] = value.reshape(RING, W, TILE)
        scatter_send(SCATTER_X, i, part2, hop2_s, plus2_s, minus2_s, hop2_r, plus2_r, minus2_r,
                     xl, xr, xo, x_plus, x_minus)

    def hop2(i):
        scatter_hop(SCATTER_X, i, part2, hop2_s, plus2_s, minus2_s, hop2_r, plus2_r, minus2_r,
                    xl, xr, x_plus, x_minus)

    def end(i):
        value = scatter_wait(SCATTER_X, i, part2, x, plus2_r, minus2_r, x_plus)

        def away():
            q = i - EARLY
            out_s[q] = value.astype(BF16)
            copy(SEND_OUT, q, out_s.at[q], out_r.at[q], far).start()

        def here():
            q = jnp.where(i < EARLY, i, i - half_chunks)
            total_v[pl.ds(pl.multiple_of(q * W, W), W), :] = value

        choose(is_far(i), away, here)

    stages = {
        "enter": enter, "relay": relay, "first": first, "merge": merge, "hop1": hop1, "to_pair": to_pair,
        "round_first": round_first, "relay2": relay2, "spread": spread, "second": second, "hop2": hop2, "end": end,
    }
    total = 1 + max(max(at_steps) for at_steps in STEPS.values())
    words = [
        [sum(1 << (t - w) for t in STEPS[name] if w <= t < w + SPAN) for w in range(0, total, SPAN)]
        for name in ORDER
    ]

    def loop(step, carry):
        bits, counts = carry
        next_bits, next_counts = [], []
        for name, word, bit, count in zip(ORDER, words, bits, counts):
            for w in range(1, len(word)):
                bit = jnp.where(step == w * SPAN, word[w], bit)
            on = bit % 2

            @pl.when(on == 1)
            def _():
                stages[name](count)

            next_bits.append(bit // 2)
            next_counts.append(count + on)
        return tuple(next_bits), tuple(next_counts)

    start = tuple(jnp.int32(word[0]) for word in words), tuple(jnp.int32(0) for _ in words)
    lax.fori_loop(0, total, loop, start)

    def store(q):
        band = pl.ds(q * W, W)
        return pltpu.make_async_copy(total_v.at[band], out.at[band], local_sem.at[2 + q])

    for q in range(half_chunks):
        copy(SEND_OUT, q, out_s.at[q], out_r.at[q], far).wait_recv()
        total_v[q * W:(q + 1) * W] += out_r[q].astype(F32)
        store(q).start()

    factor_copy(mine).wait_send()

    def sent(kind, i, piece):
        copy(kind, i, piece, piece, pair).wait_send()

    def drain(i, carry):
        for kind in (GATHER_X, SCATTER_X):
            for k in range(6):
                sent(kind + k, i, hop_s.at[i, whole, lo])

        def drain_z(part_rows):
            for kind in (GATHER_Z, SCATTER_Z):
                for k in range(6):
                    sent(kind + k, i, hop_s.at[i, part_rows, lo])

        def flipped():
            drain_z(kept)
            slot = flip_slot(i)
            sent(PRE, slot, pre_s.at[slot])
            sent(POST, slot, pre_s.at[slot])

        def plain():
            drain_z(whole)
            sent(PAIR, i, pair_s.at[i])

        choose(is_flip(i), flipped, plain)

        @pl.when(i < half_chunks)
        def _():
            sent(SEND_G, EARLY + i, pair_s.at[i])
            sent(SEND_OUT, i, out_s.at[i])

        return carry

    lax.fori_loop(0, chunks, drain, 0)
    for q in range(half_chunks):
        store(q).wait()


def local(gradient, precond):
    rows, width = gradient.shape
    chunks = 2 * rows // W
    flips = max(1, len(FLIP))
    block = pltpu.VMEM((chunks, W, width), BF16)
    ring = pltpu.VMEM((chunks, RING, W, width), BF16)
    part = pltpu.VMEM((PARTS, RING, W, width), F32)
    out_block = pltpu.VMEM((chunks // 2, W, width), BF16)
    half_ring = pltpu.VMEM((flips, RING, W // 2, width), BF16)
    square = pltpu.VMEM((2 * precond.shape[0], width), BF16)
    return pl.pallas_call(
        functools.partial(kernel, rows),
        out_shape=jax.ShapeDtypeStruct((rows, width), F32),
        in_specs=[pl.BlockSpec(memory_space=pl.ANY)] * 2,
        out_specs=pl.BlockSpec(memory_space=pl.ANY),
        scratch_shapes=[
            pltpu.VMEM((rows, width), F32),
            square, square,
            ring, part, block, block, block, block, block, block, block, block,
            ring, part, block, block, block, block, block, block,
            out_block, out_block, half_ring, half_ring,
            pltpu.VMEM((rows, width), F32),
            pltpu.SemaphoreType.DMA((2 + chunks // 2,)),
            pltpu.SemaphoreType.DMA,
            pltpu.SemaphoreType.DMA,
            pltpu.SemaphoreType.DMA((KINDS, chunks)),
            pltpu.SemaphoreType.DMA((KINDS, chunks)),
        ],
        compiler_params=pltpu.CompilerParams(
            collective_id=0, has_side_effects=True, vmem_limit_bytes=50 * 1024 * 1024
        ),
    )(gradient, precond)


def solution(mesh):
    placed = (P("row", "col"), P("row", "col"))
    return jax.shard_map(
        local, mesh=mesh, in_specs=placed, out_specs=P("row", "col"), check_vma=False
    )
```

```python
import functools

import jax
import jax.numpy as jnp
from jax import lax
from jax.experimental import pallas as pl
from jax.experimental.pallas import tpu as pltpu
from jax.sharding import PartitionSpec as P

MESH = pl.DeviceIdType.MESH
BF16, F32 = jnp.bfloat16, jnp.float32

W = 32
TILE = 256
RING = 4
EARLY = 2
FLIP = (3,)
PARTS = 4
SPAN = 30

GATHER_X, SEND_G, SCATTER_Z, PAIR, GATHER_Z, SCATTER_X, SEND_OUT, PRE, POST, KINDS = 0, 6, 7, 13, 14, 20, 26, 27, 28, 29

ORDER = (
    "enter", "to_pair", "relay", "relay2", "hop2",
    "first", "hop1", "merge", "round_first", "second",
    "end", "spread",
)
STEPS = {
    "enter": (0, 1, 2, 3, 7, 10, 11, 12),
    "to_pair": (8, 11, 12, 17, 21, 22, 25, 27),
    "relay": (1, 2, 4, 5, 9, 12, 13, 15),
    "relay2": (12, 18, 19, 20, 26, 27, 30, 31),
    "hop2": (17, 25, 27, 28, 31, 33, 36, 37),
    "first": (3, 6, 7, 8, 11, 16, 21, 22),
    "hop1": (5, 8, 9, 13, 14, 18, 23, 24),
    "merge": (12,),
    "round_first": (10, 12, 15, 23, 25, 27, 29),
    "second": (15, 21, 24, 26, 28, 29, 33, 34),
    "end": (22, 27, 31, 32, 34, 35, 37, 38),
    "spread": (22,),
}


def pick(count, items):
    value = jnp.int32(items[0])
    for k in range(1, len(items)):
        value = jnp.where(count == k, items[k], value)
    return value


def kernel(rows, g_hbm, q_hbm, out, g_wide, factor, factor_t, gath, part, hop_s, plus_s, minus_s, hop_r, plus_r,
           minus_r, pair_s, pair_r, mid, part2, hop2_s, plus2_s, minus2_s, hop2_r, plus2_r, minus2_r,
           out_s, out_r, pre_s, pre_r, total_v, local_sem, core_send, core_recv, ss, rs):
    half_chunks = rows // W
    chunks = 2 * half_chunks
    width = factor.shape[1]
    r, c = lax.axis_index("row"), lax.axis_index("col")
    core = r % 2
    x = (r // 2) % RING
    yh = r // (2 * RING)
    z = c % RING
    yl = c // RING

    def at(yh, x, core, yl, z):
        return ((yh * RING + x) * 2 + core, yl * RING + z)

    xr, xl, xo = (x + 1) % RING, (x + 3) % RING, (x + 2) % RING
    zr, zl, zo = (z + 1) % RING, (z + 3) % RING, (z + 2) % RING
    x_plus, x_minus = at(yh, xr, core, yl, z), at(yh, xl, core, yl, z)
    z_plus, z_minus = at(yh, x, core, yl, zr), at(yh, x, core, yl, zl)
    far = at(1 - yh, x, core, yl, z)
    pair = at(yh, x, core, 1 - yl, z)
    twin = at(yh, x, 1 - core, yl, z)

    depth = q_hbm.shape[0]
    mine = pl.ds(pl.multiple_of(core * depth, depth), depth)
    theirs = pl.ds(pl.multiple_of((1 - core) * depth, depth), depth)
    lo, hi = pl.ds(0, width // 2), pl.ds(width // 2, width // 2)
    whole = pl.ds(0, W)
    kept = pl.ds(pl.multiple_of(yl * (W // 2), W // 2), W // 2)
    given = pl.ds(pl.multiple_of((1 - yl) * (W // 2), W // 2), W // 2)

    load_g = pltpu.make_async_copy(g_hbm, g_wide, local_sem.at[0])
    load_q = pltpu.make_async_copy(q_hbm, factor.at[mine], local_sem.at[1])
    load_g.start()
    load_q.start()

    barrier = pltpu.get_barrier_semaphore()
    for device in (x_plus, x_minus, z_plus, z_minus, far, pair, twin):
        pl.semaphore_signal(barrier, inc=1, device_id=device, device_id_type=MESH)
    pl.semaphore_wait(barrier, 7)

    def factor_copy(side):
        return pltpu.make_async_remote_copy(
            src_ref=q_hbm, dst_ref=factor.at[side], send_sem=core_send, recv_sem=core_recv,
            device_id=twin, device_id_type=MESH)

    factor_copy(mine).start()

    def copy(kind, i, src, dst, device):
        return pltpu.make_async_remote_copy(
            src_ref=src, dst_ref=dst, send_sem=ss.at[kind, i], recv_sem=rs.at[kind, i],
            device_id=device, device_id_type=MESH)

    def gather_send(kind, i, buf, me, plus, minus, part_rows=whole):
        for k, cols, device in ((0, lo, plus), (1, hi, minus), (2, hi, plus), (3, lo, minus)):
            piece = buf.at[i, me, part_rows, cols]
            copy(kind + k, i, piece, piece, device).start()

    def gather_relay(kind, i, buf, left, right, plus, minus, part_rows=whole):
        for k, block, cols, device in ((0, left, lo, plus), (1, right, hi, minus)):
            piece = buf.at[i, block, part_rows, cols]
            copy(kind + k, i, piece, piece, device).wait_recv()
            copy(kind + 4 + k, i, piece, piece, device).start()

    def gather_wait(kind, i, buf, left, right, across, plus, minus, part_rows=whole):
        for k, block, cols in ((2, left, hi), (3, right, lo), (4, across, lo), (5, across, hi)):
            piece = buf.at[i, block, part_rows, cols]
            copy(kind + k, i, piece, piece, plus).wait_recv()

    def scatter_send(kind, i, p, hs, ps, ms, hr, pr, mr, left, right, across, plus, minus, part_rows=whole):
        hs[i, part_rows] = p[i % PARTS, across, part_rows].astype(BF16)
        copy(kind, i, hs.at[i, part_rows, lo], hr.at[i, part_rows, lo], plus).start()
        copy(kind + 1, i, hs.at[i, part_rows, hi], hr.at[i, part_rows, hi], minus).start()
        ps[i, part_rows, hi] = p[i % PARTS, right, part_rows, hi].astype(BF16)
        copy(kind + 2, i, ps.at[i, part_rows, hi], pr.at[i, part_rows, hi], plus).start()
        ms[i, part_rows, lo] = p[i % PARTS, left, part_rows, lo].astype(BF16)
        copy(kind + 3, i, ms.at[i, part_rows, lo], mr.at[i, part_rows, lo], minus).start()

    def scatter_hop(kind, i, p, hs, ps, ms, hr, pr, mr, left, right, plus, minus, part_rows=whole):
        copy(kind, i, hs.at[i, part_rows, lo], hr.at[i, part_rows, lo], plus).wait_recv()
        ps[i, part_rows, lo] = (p[i % PARTS, right, part_rows, lo] + hr[i, part_rows, lo].astype(F32)).astype(BF16)
        copy(kind + 4, i, ps.at[i, part_rows, lo], pr.at[i, part_rows, lo], plus).start()
        copy(kind + 1, i, hs.at[i, part_rows, hi], hr.at[i, part_rows, hi], minus).wait_recv()
        ms[i, part_rows, hi] = (p[i % PARTS, left, part_rows, hi] + hr[i, part_rows, hi].astype(F32)).astype(BF16)
        copy(kind + 5, i, ms.at[i, part_rows, hi], mr.at[i, part_rows, hi], minus).start()

    def scatter_wait(kind, i, p, me, pr, mr, plus, part_rows=whole):
        for k, buf, cols in ((2, pr, hi), (3, mr, lo), (4, pr, lo), (5, mr, hi)):
            piece = buf.at[i, part_rows, cols]
            copy(kind + k, i, piece, piece, plus).wait_recv()
        return p[i % PARTS, me, part_rows] + pr[i, part_rows].astype(F32) + mr[i, part_rows].astype(F32)

    def is_far(i):
        return (i >= EARLY) & (i < EARLY + half_chunks)

    def is_flip(i):
        flag = i < 0
        for f in FLIP:
            flag = flag | (i == f)
        return flag

    def flip_slot(i):
        slot = jnp.int32(0)
        for f in FLIP[1:]:
            slot = slot + (i >= f).astype(jnp.int32)
        return slot

    def choose(flag, yes, no):
        pl.when(flag)(yes)
        pl.when(jnp.logical_not(flag))(no)

    load_g.wait()
    for q in range(half_chunks):
        i = q if q < EARLY else half_chunks + q
        gath[i, x] = g_wide[q * W:(q + 1) * W].astype(BF16)
        if i == 0:
            gather_send(GATHER_X, i, gath, x, x_plus, x_minus)
        copy(SEND_G, EARLY + q, gath.at[i, x], gath.at[EARLY + q, x], far).start()
    load_q.wait()
    factor_t[:, mine] = factor[mine, :].T

    def enter(i):
        @pl.when(is_far(i))
        def _():
            copy(SEND_G, i, gath.at[i, x], gath.at[i, x], far).wait_recv()

        @pl.when(i > 0)
        def _():
            gather_send(GATHER_X, i, gath, x, x_plus, x_minus)

    def relay(i):
        gather_relay(GATHER_X, i, gath, xl, xr, x_plus, x_minus)

    def z_send(i, part_rows):
        scatter_send(SCATTER_Z, i, part, hop_s, plus_s, minus_s, hop_r, plus_r, minus_r,
                     zl, zr, zo, z_plus, z_minus, part_rows)

    def first(i):
        gather_wait(GATHER_X, i, gath, xl, xr, xo, x_plus, x_minus)

        @pl.when(i == 0)
        def _():
            lhs = gath[0].reshape(RING * W, width)
            for t in range(0, depth, 256):
                tile = min(256, depth - t)
                cols = pl.ds(pl.multiple_of(core * depth + t, 128), tile)
                value = jnp.dot(lhs, factor_t[:, cols], preferred_element_type=F32)
                part[0, :, :, cols] = value.reshape(RING, W, tile)
            factor_copy(theirs).wait_recv()
            for t in range(0, depth, 256):
                tile = min(256, depth - t)
                cols = pl.ds(pl.multiple_of((1 - core) * depth + t, 128), tile)
                value = lax.dot_general(
                    lhs, factor[cols, :], (((1,), (1,)), ((), ())), preferred_element_type=F32)
                part[0, :, :, cols] = value.reshape(RING, W, tile)
            z_send(0, whole)
            factor_t[:, theirs] = factor[theirs, :].T

        @pl.when(i > 0)
        def _():
            lhs = gath[i].reshape(RING * W, width)
            for t in range(0, width, TILE):
                value = jnp.dot(lhs, factor_t[:, t:t + TILE], preferred_element_type=F32)
                part[i % PARTS, :, :, t:t + TILE] = value.reshape(RING, W, TILE)

            def exchange():
                slot = flip_slot(i)
                pre_s[slot] = part[i % PARTS, :, given].astype(BF16)
                copy(PRE, slot, pre_s.at[slot], pre_r.at[slot], pair).start()

            choose(is_flip(i), exchange, lambda: z_send(i, whole))

    def merge(count):
        i = pick(count, FLIP)
        copy(PRE, count, pre_s.at[count], pre_r.at[count], pair).wait_recv()
        part[i % PARTS, :, kept] += pre_r[count].astype(F32)
        z_send(i, kept)

    def hop1(i):
        def run(part_rows):
            scatter_hop(SCATTER_Z, i, part, hop_s, plus_s, minus_s, hop_r, plus_r, minus_r,
                        zl, zr, z_plus, z_minus, part_rows)

        choose(is_flip(i), lambda: run(kept), lambda: run(whole))

    def to_pair(i):
        def flipped():
            value = scatter_wait(SCATTER_Z, i, part, z, plus_r, minus_r, z_plus, kept)
            mid[i, z, kept] = value.astype(BF16)
            gather_send(GATHER_Z, i, mid, z, z_plus, z_minus, kept)

        def plain():
            value = scatter_wait(SCATTER_Z, i, part, z, plus_r, minus_r, z_plus)
            part[i % PARTS, z] = value
            pair_s[i] = value.astype(BF16)
            copy(PAIR, i, pair_s.at[i], pair_r.at[i], pair).start()

        choose(is_flip(i), flipped, plain)

    def round_first(count):
        i = pick(count, [k for k in range(chunks) if k not in FLIP])
        copy(PAIR, i, pair_s.at[i], pair_r.at[i], pair).wait_recv()
        mid[i, z] = (part[i % PARTS, z] + pair_r[i].astype(F32)).astype(BF16)
        gather_send(GATHER_Z, i, mid, z, z_plus, z_minus)

    def relay2(i):
        def run(part_rows):
            gather_relay(GATHER_Z, i, mid, zl, zr, z_plus, z_minus, part_rows)

        choose(is_flip(i), lambda: run(kept), lambda: run(whole))

    def spread(count):
        i = pick(count, FLIP)
        gather_wait(GATHER_Z, i, mid, zl, zr, zo, z_plus, z_minus, kept)
        copy(POST, count, mid.at[i, :, kept], mid.at[i, :, kept], pair).start()

    def second(i):
        def flipped():
            piece = mid.at[i, :, given]
            copy(POST, flip_slot(i), piece, piece, pair).wait_recv()

        choose(is_flip(i), flipped, lambda: gather_wait(GATHER_Z, i, mid, zl, zr, zo, z_plus, z_minus))
        lhs = mid[i].reshape(RING * W, width)
        for t in range(0, width, TILE):
            value = jnp.dot(lhs, factor[:, t:t + TILE], preferred_element_type=F32)
            part2[i % PARTS, :, :, t:t + TILE] = value.reshape(RING, W, TILE)
        scatter_send(SCATTER_X, i, part2, hop2_s, plus2_s, minus2_s, hop2_r, plus2_r, minus2_r,
                     xl, xr, xo, x_plus, x_minus)

    def hop2(i):
        scatter_hop(SCATTER_X, i, part2, hop2_s, plus2_s, minus2_s, hop2_r, plus2_r, minus2_r,
                    xl, xr, x_plus, x_minus)

    def end(i):
        value = scatter_wait(SCATTER_X, i, part2, x, plus2_r, minus2_r, x_plus)

        def away():
            q = i - EARLY
            out_s[q] = value.astype(BF16)
            copy(SEND_OUT, q, out_s.at[q], out_r.at[q], far).start()

        def here():
            q = jnp.where(i < EARLY, i, i - half_chunks)
            total_v[pl.ds(pl.multiple_of(q * W, W), W), :] = value

        choose(is_far(i), away, here)

    stages = {
        "enter": enter, "relay": relay, "first": first, "merge": merge, "hop1": hop1, "to_pair": to_pair,
        "round_first": round_first, "relay2": relay2, "spread": spread, "second": second, "hop2": hop2, "end": end,
    }
    total = 1 + max(max(at_steps) for at_steps in STEPS.values())
    words = [
        [sum(1 << (t - w) for t in STEPS[name] if w <= t < w + SPAN) for w in range(0, total, SPAN)]
        for name in ORDER
    ]

    def loop(step, carry):
        bits, counts = carry
        next_bits, next_counts = [], []
        for name, word, bit, count in zip(ORDER, words, bits, counts):
            for w in range(1, len(word)):
                bit = jnp.where(step == w * SPAN, word[w], bit)
            on = bit % 2

            @pl.when(on == 1)
            def _():
                stages[name](count)

            next_bits.append(bit // 2)
            next_counts.append(count + on)
        return tuple(next_bits), tuple(next_counts)

    start = tuple(jnp.int32(word[0]) for word in words), tuple(jnp.int32(0) for _ in words)
    lax.fori_loop(0, total, loop, start)

    def store(q):
        band = pl.ds(q * W, W)
        return pltpu.make_async_copy(total_v.at[band], out.at[band], local_sem.at[2 + q])

    for q in range(half_chunks):
        copy(SEND_OUT, q, out_s.at[q], out_r.at[q], far).wait_recv()
        total_v[q * W:(q + 1) * W] += out_r[q].astype(F32)
        store(q).start()

    factor_copy(mine).wait_send()

    def sent(kind, i, piece):
        copy(kind, i, piece, piece, pair).wait_send()

    def drain(i, carry):
        for kind in (GATHER_X, SCATTER_X):
            for k in range(6):
                sent(kind + k, i, hop_s.at[i, whole, lo])

        def drain_z(part_rows):
            for kind in (GATHER_Z, SCATTER_Z):
                for k in range(6):
                    sent(kind + k, i, hop_s.at[i, part_rows, lo])

        def flipped():
            drain_z(kept)
            slot = flip_slot(i)
            sent(PRE, slot, pre_s.at[slot])
            sent(POST, slot, pre_s.at[slot])

        def plain():
            drain_z(whole)
            sent(PAIR, i, pair_s.at[i])

        choose(is_flip(i), flipped, plain)

        @pl.when(i < half_chunks)
        def _():
            sent(SEND_G, EARLY + i, pair_s.at[i])
            sent(SEND_OUT, i, out_s.at[i])

        return carry

    lax.fori_loop(0, chunks, drain, 0)
    for q in range(half_chunks):
        store(q).wait()


def local(gradient, precond):
    rows, width = gradient.shape
    chunks = 2 * rows // W
    flips = max(1, len(FLIP))
    block = pltpu.VMEM((chunks, W, width), BF16)
    ring = pltpu.VMEM((chunks, RING, W, width), BF16)
    part = pltpu.VMEM((PARTS, RING, W, width), F32)
    out_block = pltpu.VMEM((chunks // 2, W, width), BF16)
    half_ring = pltpu.VMEM((flips, RING, W // 2, width), BF16)
    square = pltpu.VMEM((2 * precond.shape[0], width), BF16)
    return pl.pallas_call(
        functools.partial(kernel, rows),
        out_shape=jax.ShapeDtypeStruct((rows, width), F32),
        in_specs=[pl.BlockSpec(memory_space=pl.ANY)] * 2,
        out_specs=pl.BlockSpec(memory_space=pl.ANY),
        scratch_shapes=[
            pltpu.VMEM((rows, width), F32),
            square, square,
            ring, part, block, block, block, block, block, block, block, block,
            ring, part, block, block, block, block, block, block,
            out_block, out_block, half_ring, half_ring,
            pltpu.VMEM((rows, width), F32),
            pltpu.SemaphoreType.DMA((2 + chunks // 2,)),
            pltpu.SemaphoreType.DMA,
            pltpu.SemaphoreType.DMA,
            pltpu.SemaphoreType.DMA((KINDS, chunks)),
            pltpu.SemaphoreType.DMA((KINDS, chunks)),
        ],
        compiler_params=pltpu.CompilerParams(
            collective_id=0, has_side_effects=True, vmem_limit_bytes=53 * 1024 * 1024
        ),
    )(gradient, precond)


def solution(mesh):
    placed = (P("row", "col"), P("row", "col"))
    return jax.shard_map(
        local, mesh=mesh, in_specs=placed, out_specs=P("row", "col"), check_vma=False
    )
```

```python
import functools

import jax
import jax.numpy as jnp
from jax import lax
from jax.experimental import pallas as pl
from jax.experimental.pallas import tpu as pltpu
from jax.sharding import PartitionSpec as P

MESH = pl.DeviceIdType.MESH
BF16, F32 = jnp.bfloat16, jnp.float32

W = 32
TILE = 256
RING = 4
EARLY = 2
FLIP = (3,)
PARTS = 4
SPAN = 30

GATHER_X, SEND_G, SCATTER_Z, PAIR, GATHER_Z, SCATTER_X, SEND_OUT, PRE, POST, KINDS = 0, 6, 7, 13, 14, 20, 26, 27, 28, 29

ORDER = (
    "enter", "to_pair", "relay", "relay2", "hop2",
    "first", "hop1", "merge", "round_first", "second",
    "end", "spread",
)
STEPS = {
    "enter": (0, 1, 2, 3, 7, 10, 11, 12),
    "to_pair": (8, 11, 12, 17, 21, 22, 25, 27),
    "relay": (1, 2, 4, 5, 9, 12, 13, 15),
    "relay2": (12, 18, 19, 20, 26, 27, 30, 31),
    "hop2": (17, 25, 27, 28, 31, 33, 36, 37),
    "first": (3, 6, 7, 8, 11, 16, 21, 22),
    "hop1": (5, 8, 9, 13, 14, 18, 23, 24),
    "merge": (12,),
    "round_first": (10, 12, 15, 23, 25, 27, 29),
    "second": (15, 21, 24, 26, 28, 29, 33, 34),
    "end": (22, 27, 31, 32, 34, 35, 37, 38),
    "spread": (22,),
}


def pick(count, items):
    value = jnp.int32(items[0])
    for k in range(1, len(items)):
        value = jnp.where(count == k, items[k], value)
    return value


def kernel(rows, g_hbm, q_hbm, out, g_wide, factor, factor_t, gath, part, hop_s, plus_s, minus_s, hop_r, plus_r,
           minus_r, pair_s, pair_r, mid, part2, hop2_s, plus2_s, minus2_s, hop2_r, plus2_r, minus2_r,
           out_s, out_r, pre_s, pre_r, total_v, local_sem, core_send, core_recv, ss, rs):
    half_chunks = rows // W
    chunks = 2 * half_chunks
    width = factor.shape[1]
    r, c = lax.axis_index("row"), lax.axis_index("col")
    core = r % 2
    x = (r // 2) % RING
    yh = r // (2 * RING)
    z = c % RING
    yl = c // RING

    def at(yh, x, core, yl, z):
        return ((yh * RING + x) * 2 + core, yl * RING + z)

    xr, xl, xo = (x + 1) % RING, (x + 3) % RING, (x + 2) % RING
    zr, zl, zo = (z + 1) % RING, (z + 3) % RING, (z + 2) % RING
    x_plus, x_minus = at(yh, xr, core, yl, z), at(yh, xl, core, yl, z)
    z_plus, z_minus = at(yh, x, core, yl, zr), at(yh, x, core, yl, zl)
    far = at(1 - yh, x, core, yl, z)
    pair = at(yh, x, core, 1 - yl, z)
    twin = at(yh, x, 1 - core, yl, z)

    depth = q_hbm.shape[0]
    mine = pl.ds(pl.multiple_of(core * depth, depth), depth)
    theirs = pl.ds(pl.multiple_of((1 - core) * depth, depth), depth)
    lo, hi = pl.ds(0, width // 2), pl.ds(width // 2, width // 2)
    whole = pl.ds(0, W)
    kept = pl.ds(pl.multiple_of(yl * (W // 2), W // 2), W // 2)
    given = pl.ds(pl.multiple_of((1 - yl) * (W // 2), W // 2), W // 2)

    load_g = pltpu.make_async_copy(g_hbm, g_wide, local_sem.at[0])
    load_q = pltpu.make_async_copy(q_hbm, factor.at[mine], local_sem.at[1])
    load_g.start()
    load_q.start()

    barrier = pltpu.get_barrier_semaphore()
    for device in (x_plus, x_minus, z_plus, z_minus, far, pair, twin):
        pl.semaphore_signal(barrier, inc=1, device_id=device, device_id_type=MESH)
    pl.semaphore_wait(barrier, 7)

    def factor_copy(side):
        return pltpu.make_async_remote_copy(
            src_ref=q_hbm, dst_ref=factor.at[side], send_sem=core_send, recv_sem=core_recv,
            device_id=twin, device_id_type=MESH)

    factor_copy(mine).start()

    def copy(kind, i, src, dst, device):
        return pltpu.make_async_remote_copy(
            src_ref=src, dst_ref=dst, send_sem=ss.at[kind, i], recv_sem=rs.at[kind, i],
            device_id=device, device_id_type=MESH)

    def gather_send(kind, i, buf, me, plus, minus, part_rows=whole):
        for k, cols, device in ((0, lo, plus), (1, hi, minus), (2, hi, plus), (3, lo, minus)):
            piece = buf.at[i, me, part_rows, cols]
            copy(kind + k, i, piece, piece, device).start()

    def gather_relay(kind, i, buf, left, right, plus, minus, part_rows=whole):
        for k, block, cols, device in ((0, left, lo, plus), (1, right, hi, minus)):
            piece = buf.at[i, block, part_rows, cols]
            copy(kind + k, i, piece, piece, device).wait_recv()
            copy(kind + 4 + k, i, piece, piece, device).start()

    def gather_wait(kind, i, buf, left, right, across, plus, minus, part_rows=whole):
        for k, block, cols in ((2, left, hi), (3, right, lo), (4, across, lo), (5, across, hi)):
            piece = buf.at[i, block, part_rows, cols]
            copy(kind + k, i, piece, piece, plus).wait_recv()

    def scatter_send(kind, i, p, hs, ps, ms, hr, pr, mr, left, right, across, plus, minus, part_rows=whole):
        hs[i, part_rows] = p[i % PARTS, across, part_rows].astype(BF16)
        copy(kind, i, hs.at[i, part_rows, lo], hr.at[i, part_rows, lo], plus).start()
        copy(kind + 1, i, hs.at[i, part_rows, hi], hr.at[i, part_rows, hi], minus).start()
        ps[i, part_rows, hi] = p[i % PARTS, right, part_rows, hi].astype(BF16)
        copy(kind + 2, i, ps.at[i, part_rows, hi], pr.at[i, part_rows, hi], plus).start()
        ms[i, part_rows, lo] = p[i % PARTS, left, part_rows, lo].astype(BF16)
        copy(kind + 3, i, ms.at[i, part_rows, lo], mr.at[i, part_rows, lo], minus).start()

    def scatter_hop(kind, i, p, hs, ps, ms, hr, pr, mr, left, right, plus, minus, part_rows=whole):
        copy(kind, i, hs.at[i, part_rows, lo], hr.at[i, part_rows, lo], plus).wait_recv()
        ps[i, part_rows, lo] = (p[i % PARTS, right, part_rows, lo] + hr[i, part_rows, lo].astype(F32)).astype(BF16)
        copy(kind + 4, i, ps.at[i, part_rows, lo], pr.at[i, part_rows, lo], plus).start()
        copy(kind + 1, i, hs.at[i, part_rows, hi], hr.at[i, part_rows, hi], minus).wait_recv()
        ms[i, part_rows, hi] = (p[i % PARTS, left, part_rows, hi] + hr[i, part_rows, hi].astype(F32)).astype(BF16)
        copy(kind + 5, i, ms.at[i, part_rows, hi], mr.at[i, part_rows, hi], minus).start()

    def scatter_wait(kind, i, p, me, pr, mr, plus, part_rows=whole):
        for k, buf, cols in ((2, pr, hi), (3, mr, lo), (4, pr, lo), (5, mr, hi)):
            piece = buf.at[i, part_rows, cols]
            copy(kind + k, i, piece, piece, plus).wait_recv()
        return p[i % PARTS, me, part_rows] + pr[i, part_rows].astype(F32) + mr[i, part_rows].astype(F32)

    def is_far(i):
        return (i >= EARLY) & (i < EARLY + half_chunks)

    def is_flip(i):
        flag = i < 0
        for f in FLIP:
            flag = flag | (i == f)
        return flag

    def flip_slot(i):
        slot = jnp.int32(0)
        for f in FLIP[1:]:
            slot = slot + (i >= f).astype(jnp.int32)
        return slot

    def choose(flag, yes, no):
        pl.when(flag)(yes)
        pl.when(jnp.logical_not(flag))(no)

    def sent(kind, i, piece):
        copy(kind, i, piece, piece, pair).wait_send()

    def drain(i):
        for kind in (GATHER_X, SCATTER_X):
            for k in range(6):
                sent(kind + k, i, hop_s.at[i, whole, lo])

        def drain_z(part_rows):
            for kind in (GATHER_Z, SCATTER_Z):
                for k in range(6):
                    sent(kind + k, i, hop_s.at[i, part_rows, lo])

        def flipped():
            drain_z(kept)
            slot = flip_slot(i)
            sent(PRE, slot, pre_s.at[slot])
            sent(POST, slot, pre_s.at[slot])

        def plain():
            drain_z(whole)
            sent(PAIR, i, pair_s.at[i])

        choose(is_flip(i), flipped, plain)

        @pl.when(is_far(i))
        def _():
            sent(SEND_G, i, pair_s.at[i])

    load_g.wait()
    for q in range(half_chunks):
        i = q if q < EARLY else half_chunks + q
        gath[i, x] = g_wide[q * W:(q + 1) * W].astype(BF16)
        if i == 0:
            gather_send(GATHER_X, i, gath, x, x_plus, x_minus)
        copy(SEND_G, EARLY + q, gath.at[i, x], gath.at[EARLY + q, x], far).start()
    load_q.wait()
    factor_t[:, mine] = factor[mine, :].T

    def enter(i):
        @pl.when(is_far(i))
        def _():
            copy(SEND_G, i, gath.at[i, x], gath.at[i, x], far).wait_recv()

        @pl.when(i > 0)
        def _():
            gather_send(GATHER_X, i, gath, x, x_plus, x_minus)

    def relay(i):
        gather_relay(GATHER_X, i, gath, xl, xr, x_plus, x_minus)

    def z_send(i, part_rows):
        scatter_send(SCATTER_Z, i, part, hop_s, plus_s, minus_s, hop_r, plus_r, minus_r,
                     zl, zr, zo, z_plus, z_minus, part_rows)

    def first(i):
        gather_wait(GATHER_X, i, gath, xl, xr, xo, x_plus, x_minus)

        @pl.when(i == 0)
        def _():
            lhs = gath[0].reshape(RING * W, width)
            for t in range(0, depth, 256):
                tile = min(256, depth - t)
                cols = pl.ds(pl.multiple_of(core * depth + t, 128), tile)
                value = jnp.dot(lhs, factor_t[:, cols], preferred_element_type=F32)
                part[0, :, :, cols] = value.reshape(RING, W, tile)
            factor_copy(theirs).wait_recv()
            for t in range(0, depth, 256):
                tile = min(256, depth - t)
                cols = pl.ds(pl.multiple_of((1 - core) * depth + t, 128), tile)
                value = lax.dot_general(
                    lhs, factor[cols, :], (((1,), (1,)), ((), ())), preferred_element_type=F32)
                part[0, :, :, cols] = value.reshape(RING, W, tile)
            z_send(0, whole)
            factor_t[:, theirs] = factor[theirs, :].T

        @pl.when(i > 0)
        def _():
            lhs = gath[i].reshape(RING * W, width)
            for t in range(0, width, TILE):
                value = jnp.dot(lhs, factor_t[:, t:t + TILE], preferred_element_type=F32)
                part[i % PARTS, :, :, t:t + TILE] = value.reshape(RING, W, TILE)

            def exchange():
                slot = flip_slot(i)
                pre_s[slot] = part[i % PARTS, :, given].astype(BF16)
                copy(PRE, slot, pre_s.at[slot], pre_r.at[slot], pair).start()

            choose(is_flip(i), exchange, lambda: z_send(i, whole))

    def merge(count):
        i = pick(count, FLIP)
        copy(PRE, count, pre_s.at[count], pre_r.at[count], pair).wait_recv()
        part[i % PARTS, :, kept] += pre_r[count].astype(F32)
        z_send(i, kept)

    def hop1(i):
        def run(part_rows):
            scatter_hop(SCATTER_Z, i, part, hop_s, plus_s, minus_s, hop_r, plus_r, minus_r,
                        zl, zr, z_plus, z_minus, part_rows)

        choose(is_flip(i), lambda: run(kept), lambda: run(whole))

    def to_pair(i):
        def flipped():
            value = scatter_wait(SCATTER_Z, i, part, z, plus_r, minus_r, z_plus, kept)
            mid[i, z, kept] = value.astype(BF16)
            gather_send(GATHER_Z, i, mid, z, z_plus, z_minus, kept)

        def plain():
            value = scatter_wait(SCATTER_Z, i, part, z, plus_r, minus_r, z_plus)
            part[i % PARTS, z] = value
            pair_s[i] = value.astype(BF16)
            copy(PAIR, i, pair_s.at[i], pair_r.at[i], pair).start()

        choose(is_flip(i), flipped, plain)

    def round_first(count):
        i = pick(count, [k for k in range(chunks) if k not in FLIP])
        copy(PAIR, i, pair_s.at[i], pair_r.at[i], pair).wait_recv()
        mid[i, z] = (part[i % PARTS, z] + pair_r[i].astype(F32)).astype(BF16)
        gather_send(GATHER_Z, i, mid, z, z_plus, z_minus)

    def relay2(i):
        def run(part_rows):
            gather_relay(GATHER_Z, i, mid, zl, zr, z_plus, z_minus, part_rows)

        choose(is_flip(i), lambda: run(kept), lambda: run(whole))

    def spread(count):
        i = pick(count, FLIP)
        gather_wait(GATHER_Z, i, mid, zl, zr, zo, z_plus, z_minus, kept)
        copy(POST, count, mid.at[i, :, kept], mid.at[i, :, kept], pair).start()

    def second(i):
        def flipped():
            piece = mid.at[i, :, given]
            copy(POST, flip_slot(i), piece, piece, pair).wait_recv()

        choose(is_flip(i), flipped, lambda: gather_wait(GATHER_Z, i, mid, zl, zr, zo, z_plus, z_minus))
        lhs = mid[i].reshape(RING * W, width)
        for t in range(0, width, TILE):
            value = jnp.dot(lhs, factor[:, t:t + TILE], preferred_element_type=F32)
            part2[i % PARTS, :, :, t:t + TILE] = value.reshape(RING, W, TILE)
        scatter_send(SCATTER_X, i, part2, hop2_s, plus2_s, minus2_s, hop2_r, plus2_r, minus2_r,
                     xl, xr, xo, x_plus, x_minus)

    def hop2(i):
        scatter_hop(SCATTER_X, i, part2, hop2_s, plus2_s, minus2_s, hop2_r, plus2_r, minus2_r,
                    xl, xr, x_plus, x_minus)

    def end(i):
        value = scatter_wait(SCATTER_X, i, part2, x, plus2_r, minus2_r, x_plus)

        def away():
            q = i - EARLY
            out_s[q] = value.astype(BF16)
            copy(SEND_OUT, q, out_s.at[q], out_r.at[q], far).start()

        def here():
            q = jnp.where(i < EARLY, i, i - half_chunks)
            total_v[pl.ds(pl.multiple_of(q * W, W), W), :] = value

        choose(is_far(i), away, here)

        @pl.when(i > 0)
        def _():
            drain(i - 1)

    stages = {
        "enter": enter, "relay": relay, "first": first, "merge": merge, "hop1": hop1, "to_pair": to_pair,
        "round_first": round_first, "relay2": relay2, "spread": spread, "second": second, "hop2": hop2, "end": end,
    }
    total = 1 + max(max(at_steps) for at_steps in STEPS.values())
    words = [
        [sum(1 << (t - w) for t in STEPS[name] if w <= t < w + SPAN) for w in range(0, total, SPAN)]
        for name in ORDER
    ]

    def loop(step, carry):
        bits, counts = carry
        next_bits, next_counts = [], []
        for name, word, bit, count in zip(ORDER, words, bits, counts):
            for w in range(1, len(word)):
                bit = jnp.where(step == w * SPAN, word[w], bit)
            on = bit % 2

            @pl.when(on == 1)
            def _():
                stages[name](count)

            next_bits.append(bit // 2)
            next_counts.append(count + on)
        return tuple(next_bits), tuple(next_counts)

    start = tuple(jnp.int32(word[0]) for word in words), tuple(jnp.int32(0) for _ in words)
    lax.fori_loop(0, total, loop, start)

    def store(q):
        band = pl.ds(q * W, W)
        return pltpu.make_async_copy(total_v.at[band], out.at[band], local_sem.at[2 + q])

    for q in range(half_chunks):
        copy(SEND_OUT, q, out_s.at[q], out_r.at[q], far).wait_recv()
        total_v[q * W:(q + 1) * W] += out_r[q].astype(F32)
        store(q).start()

    factor_copy(mine).wait_send()

    drain(jnp.int32(chunks - 1))
    for q in range(half_chunks):
        sent(SEND_OUT, q, out_s.at[q])
    for q in range(half_chunks):
        store(q).wait()


def local(gradient, precond):
    rows, width = gradient.shape
    chunks = 2 * rows // W
    flips = max(1, len(FLIP))
    block = pltpu.VMEM((chunks, W, width), BF16)
    ring = pltpu.VMEM((chunks, RING, W, width), BF16)
    part = pltpu.VMEM((PARTS, RING, W, width), F32)
    out_block = pltpu.VMEM((chunks // 2, W, width), BF16)
    half_ring = pltpu.VMEM((flips, RING, W // 2, width), BF16)
    square = pltpu.VMEM((2 * precond.shape[0], width), BF16)
    return pl.pallas_call(
        functools.partial(kernel, rows),
        out_shape=jax.ShapeDtypeStruct((rows, width), F32),
        in_specs=[pl.BlockSpec(memory_space=pl.ANY)] * 2,
        out_specs=pl.BlockSpec(memory_space=pl.ANY),
        scratch_shapes=[
            pltpu.VMEM((rows, width), F32),
            square, square,
            ring, part, block, block, block, block, block, block, block, block,
            ring, part, block, block, block, block, block, block,
            out_block, out_block, half_ring, half_ring,
            pltpu.VMEM((rows, width), F32),
            pltpu.SemaphoreType.DMA((2 + chunks // 2,)),
            pltpu.SemaphoreType.DMA,
            pltpu.SemaphoreType.DMA,
            pltpu.SemaphoreType.DMA((KINDS, chunks)),
            pltpu.SemaphoreType.DMA((KINDS, chunks)),
        ],
        compiler_params=pltpu.CompilerParams(
            collective_id=0, has_side_effects=True, vmem_limit_bytes=53 * 1024 * 1024
        ),
    )(gradient, precond)


def solution(mesh):
    placed = (P("row", "col"), P("row", "col"))
    return jax.shard_map(
        local, mesh=mesh, in_specs=placed, out_specs=P("row", "col"), check_vma=False
    )
```
